32 devices in a mesh: item: 2 (over core), site: 16 (over z, y, x).
Axes of the slice: x: 2, y: 2, z: 4, core: 2. Of those that a mesh axis runs over, the one named last changes fastest.
Arguments:
- item_factors: float32 [16, 32, 65536], P('site', None, 'item'), may hold values from -3 to 3
- user_factors: float32 [16, 32, 4096], P('site', None, 'item'), may hold values from -3 to 3
- ratings: bfloat16 [16, 2, 128, 128, 128], P('site', 'item'), may hold values from -6 to 6
- block_rows: int32 [16, 2, 128], P('site', 'item'), may hold values from 0 to 255, as said below
- block_cols: int32 [16, 2, 128], P('site', 'item'), may hold values from 0 to 31
- block_count: int32 [16, 2], P('site', 'item'), may hold values from 16 to 128, as said below
- hop_steps: int32 [2], replicated, may hold values from 0 to 2, as said below
Outputs:
- items_out: float32 [16, 32, 65536], P('site', None, 'item')
- users_out: float32 [16, 32, 4096], P('site', None, 'item')
The draws below stay inside these ranges and needn't reach their ends.
Inputs may be any that keep to these rules, and one draw needn't show every extreme that they name: `block_rows`: within one device the live and empty slots name distinct pairs of blocks. `block_count`: some device has all 128 slots live. `hop_steps`: the steps' exponents differ.
All inputs are finite; a program needn't handle non-finite values.
Results may differ from the reference program's by a relative error of at most 0.0003.
Values sent between devices are 32-bit elements; how exact they have to be, the bound alone decides.
A program may use at most 128 MiB of HBM per device.

```python
import jax
import jax.numpy as jnp
from jax import lax

ITEMS = 65536
R = 32
BLK = 128
NB = 128
ITERS = 2
ITEM_DEV = 32768
USERS = 4096
ROW_BLOCKS = 256
COL_BLOCKS = 32
N_ITEM = 2
N_SITE = 16


def block_pairs(key):
    device_keys = jax.random.split(jax.random.fold_in(key, 17), N_SITE * N_ITEM)

    def device_pairs(device_key):
        return jax.random.permutation(device_key, ROW_BLOCKS * COL_BLOCKS)[:NB]
    paired = jax.vmap(device_pairs)(device_keys).astype(jnp.int32)
    return paired.reshape(N_SITE, N_ITEM, NB)


def draw_block_rows(key, part):
    return (block_pairs(key) // COL_BLOCKS).astype(jnp.int32)


def draw_block_cols(key, part):
    return (block_pairs(key) % COL_BLOCKS).astype(jnp.int32)


def draw_block_count(key, part):
    shrink = jax.random.randint(jax.random.fold_in(key, 5), (N_SITE * N_ITEM,), 0, 4)
    totals = NB // jnp.left_shift(jnp.int32(1), shrink.astype(jnp.int32))
    busiest = jax.random.randint(jax.random.fold_in(key, 9), (), 0, N_SITE * N_ITEM)
    totals = totals.at[busiest].set(NB)
    return totals.reshape(N_SITE, N_ITEM).astype(jnp.int32)


def draw_hop_steps(key, part):
    exponents = jnp.array([0, 2, 1], dtype=jnp.int32)[:ITERS]
    return jax.random.permutation(jax.random.fold_in(key, 3), exponents).astype(jnp.int32)


def level_of(stream_key, dims, shards, least, top_value):
    def one(dim, shards_of):
        draws = jax.random.uniform(jax.random.fold_in(jax.random.fold_in(stream_key, 6), dim), (shards_of,), jnp.float32, least / len(shards), top_value / len(shards))
        return jnp.repeat(jnp.exp(draws), dims[dim] // shards_of).reshape((-1,) + (1,) * (len(dims) - dim - 1))

    factor_of = one(*shards[0])
    for cut in shards[1:]:
        factor_of = factor_of * one(*cut)
    return factor_of


def gaussian(own_key, shape, scale, most, cuts=(), kind=jnp.bfloat16):
    result = jax.random.normal(own_key, shape, jnp.float32) * scale
    if len(cuts) > 0:
        result = level_of(own_key, shape, cuts, -0.22, 0.18) * result
    return jnp.clip(result, min=-most, max=most).astype(kind)


def setup_inputs(seed: int = 0) -> dict:
    seeds = jax.random.split(jax.random.key(seed), 8)
    return {
        "item_factors": gaussian(seeds[0], (N_SITE, R, ITEMS), 0.5, 3.0, ((0, 16), (2, 2)), jnp.float32),
        "user_factors": gaussian(seeds[1], (N_SITE, R, USERS), 0.5, 3.0, ((0, 16), (2, 2)), jnp.float32),
        "ratings": gaussian(seeds[2], (N_SITE, N_ITEM, NB, BLK, BLK), 1.0, 6.0, ((0, 16), (1, 2))),
        "block_rows": draw_block_rows(jax.random.fold_in(seeds[7], 71), 0),
        "block_cols": draw_block_cols(jax.random.fold_in(seeds[7], 71), 0),
        "block_count": draw_block_count(jax.random.fold_in(seeds[7], 71), 0),
        "hop_steps": draw_hop_steps(jax.random.fold_in(seeds[7], 71), 0),
    }


LEARN_RATE = 0.05


def shard_grads(item_shard, user_site, slot_values, row_index, column_index, block_total):
    item_tiles = item_shard.reshape(R, ROW_BLOCKS, BLK)
    user_tiles = user_site.reshape(R, COL_BLOCKS, BLK)
    item_picked = jnp.transpose(item_tiles[:, row_index, :], (1, 0, 2))
    user_picked = jnp.transpose(user_tiles[:, column_index, :], (1, 0, 2))
    rebuilt = jnp.einsum("nri,nrj->nij", item_picked, user_picked, precision=lax.Precision.HIGHEST)
    live_mask = (jnp.arange(NB, dtype=jnp.int32) < block_total).astype(jnp.float32)
    clipped = jnp.clip(rebuilt - slot_values.astype(jnp.float32), -1.0, 1.0) * live_mask[:, None, None]
    item_part = jnp.einsum("nij,nrj->nri", clipped, user_picked, precision=lax.Precision.HIGHEST)
    user_part = jnp.einsum("nij,nri->nrj", clipped, item_picked, precision=lax.Precision.HIGHEST)
    item_grad = jnp.zeros((ROW_BLOCKS, R, BLK), jnp.float32).at[row_index].add(item_part)
    user_grad = jnp.zeros((COL_BLOCKS, R, BLK), jnp.float32).at[column_index].add(user_part)
    item_grad = jnp.transpose(item_grad, (1, 0, 2)).reshape(R, ITEM_DEV)
    user_grad = jnp.transpose(user_grad, (1, 0, 2)).reshape(R, USERS)
    return item_grad, user_grad


def site_grads(packed):
    item_site, user_site, slot_values, row_index, column_index, block_total = packed
    item_shards = jnp.transpose(item_site.reshape(R, N_ITEM, ITEM_DEV), (1, 0, 2))
    item_grad, user_grad = jax.vmap(shard_grads, in_axes=(0, None, 0, 0, 0, 0))(
        item_shards, user_site, slot_values, row_index, column_index, block_total)
    item_grad = jnp.transpose(item_grad, (1, 0, 2)).reshape(R, ITEMS)
    return item_grad, jnp.sum(user_grad, axis=0)


def reference(item_factors, user_factors, ratings, block_rows, block_cols, block_count, hop_steps):
    item_state = item_factors
    user_state = user_factors
    for step_index in range(ITERS):
        item_grad, user_grad = lax.map(site_grads, (item_state, user_state, ratings, block_rows, block_cols, block_count))
        peer_hop = jnp.left_shift(jnp.int32(1), hop_steps[step_index].astype(jnp.int32))
        peer_items = jnp.roll(item_state, -peer_hop, axis=0)
        item_state = 0.5 * (item_state + peer_items) - LEARN_RATE * item_grad
        user_state = user_state - LEARN_RATE * user_grad
    return item_state, user_state
```

```python
from functools import partial

import jax
import jax.numpy as jnp
from jax import lax
from jax.experimental import pallas as pl
from jax.experimental.pallas import tpu as pltpu
from jax.sharding import PartitionSpec as P

ITERS = 2
HOPS = 3
LEARN_RATE = 0.05
CHUNKS = 4
GROUP = 8


def passed_along(block, axis, distance):
    devices = range(lax.axis_size(axis))
    route = [((i - distance) % len(devices), i) for i in devices]
    return lax.ppermute(block, axis, route)


def split_high_low(values):
    high = values.astype(jnp.bfloat16)
    low = (values - high.astype(jnp.float32)).astype(jnp.bfloat16)
    return high, low


def dot_f32(lhs, rhs, lhs_dim, rhs_dim):
    return lax.dot_general(
        lhs, rhs, (((lhs_dim,), (rhs_dim,)), ((), ())), preferred_element_type=jnp.float32
    )


def grads_kernel(chunks, rows_ref, cols_ref, count_ref, *refs):
    x_refs = refs[:chunks]
    y_ref, ratings_ref = refs[chunks : chunks + 2]
    base_refs = refs[chunks + 2 : 2 * chunks + 2]
    user_ref = refs[2 * chunks + 2]
    group, tile = ratings_ref.shape[0], ratings_ref.shape[-1]
    rank = y_ref.shape[0]
    part_rank = rank // chunks
    first = pl.program_id(0) * group
    total = count_ref[0]

    @pl.when(pl.program_id(0) == 0)
    def _():
        for x_ref, base_ref in zip(x_refs, base_refs):
            base_ref[...] = 0.5 * x_ref[...]
        user_ref[...] = jnp.zeros_like(user_ref)

    @pl.when(first < total)
    def _():
        parts = []
        for k in range(group):
            row = pl.ds(pl.multiple_of(rows_ref[first + k] * tile, tile), tile)
            col = pl.ds(pl.multiple_of(cols_ref[first + k] * tile, tile), tile)
            limit = jnp.where(first + k < total, 1.0, 0.0).astype(jnp.float32)
            x = jnp.concatenate([x_ref[:, row] for x_ref in x_refs], axis=0)
            x_high, x_low = split_high_low(x)
            y_high, y_low = split_high_low(y_ref[:, col])
            rebuilt = dot_f32(
                jnp.concatenate([x_high, x_low, x_high], axis=0),
                jnp.concatenate([y_high, y_high, y_low], axis=0),
                0,
                0,
            )
            clipped = jnp.clip(rebuilt - ratings_ref[k].astype(jnp.float32), -limit, limit)
            c_high, c_low = split_high_low(clipped)
            item_pair = dot_f32(jnp.concatenate([y_high, y_low], axis=0), c_high, 1, 1)
            item_part = item_pair[:rank] + item_pair[rank:] + dot_f32(y_high, c_low, 1, 1)
            user_pair = dot_f32(jnp.concatenate([x_high, x_low], axis=0), c_high, 1, 0)
            user_part = user_pair[:rank] + user_pair[rank:] + dot_f32(x_high, c_low, 1, 0)
            parts.append((row, col, item_part, user_part))
        for row, col, item_part, user_part in parts:
            for c, base_ref in enumerate(base_refs):
                base_ref[:, row] -= LEARN_RATE * item_part[c * part_rank : (c + 1) * part_rank]
            user_ref[:, col] += user_part


def local_grads(x_parts, users_whole, slot_values, row_index, column_index, block_total):
    chunks = len(x_parts)
    slot_total, tile = slot_values.shape[0], slot_values.shape[-1]
    rank, users = users_whole.shape
    items = x_parts[0].shape[1]
    once = pl.Buffered(1)
    x_spec = pl.BlockSpec(x_parts[0].shape, lambda i, *_: (0, 0), pipeline_mode=once)
    y_spec = pl.BlockSpec((rank, users), lambda i, *_: (0, 0), pipeline_mode=once)
    outs = pl.pallas_call(
        partial(grads_kernel, chunks),
        grid_spec=pltpu.PrefetchScalarGridSpec(
            num_scalar_prefetch=3,
            grid=(slot_total // GROUP,),
            in_specs=[x_spec] * chunks
            + [y_spec, pl.BlockSpec((GROUP, tile, tile), lambda i, *_: (i, 0, 0))],
            out_specs=[x_spec] * chunks + [y_spec],
        ),
        out_shape=[jax.ShapeDtypeStruct(p.shape, jnp.float32) for p in x_parts]
        + [jax.ShapeDtypeStruct((rank, users), jnp.float32)],
        compiler_params=pltpu.CompilerParams(vmem_limit_bytes=24 << 20),
        cost_estimate=pl.CostEstimate(
            flops=18 * slot_total * tile * tile * rank,
            bytes_accessed=8 * rank * items + 2 * slot_total * tile * tile,
            transcendentals=0,
        ),
    )(row_index, column_index, block_total, *x_parts, users_whole, slot_values)
    return outs[:chunks], outs[chunks]


def two_steps(hops, item_here, user_here, slot_values, row_index, column_index, block_total):
    rank = item_here.shape[0]
    size = rank // CHUNKS
    x_parts = [item_here[c * size : (c + 1) * size] for c in range(CHUNKS)]
    for hop in hops:
        peers = [passed_along(part, "site", -(1 << hop)) for part in x_parts]
        users_whole = lax.all_gather(user_here, "item", axis=1, tiled=True)
        bases, user_grad = local_grads(
            x_parts, users_whole, slot_values, row_index, column_index, block_total
        )
        x_parts = [base + 0.5 * peer for base, peer in zip(bases, peers)]
        owned = lax.psum_scatter(user_grad, "item", scatter_dimension=1, tiled=True)
        user_here = user_here - LEARN_RATE * owned
    return jnp.concatenate(x_parts, axis=0), user_here


def per_device(item_factors, user_factors, ratings, block_rows, block_cols, block_count, hop_steps):
    pairs = [(a, b) for a in range(HOPS) for b in range(HOPS) if a != b]
    first, second = hop_steps[0], hop_steps[1]
    chosen = first * (HOPS - 1) + second - (second > first).astype(jnp.int32)
    item_here, user_here = lax.switch(
        chosen,
        [partial(two_steps, pair) for pair in pairs],
        item_factors[0],
        user_factors[0],
        ratings[0, 0],
        block_rows[0, 0],
        block_cols[0, 0],
        block_count[0],
    )
    return (item_here[None], user_here[None])


def solution(mesh):
    return jax.shard_map(
        per_device,
        mesh=mesh,
        in_specs=(
            P("site", None, "item"),
            P("site", None, "item"),
            P("site", "item", None, None, None),
            P("site", "item", None),
            P("site", "item", None),
            P("site", "item"),
            P(),
        ),
        out_specs=(P("site", None, "item"), P("site", None, "item")),
        check_vma=False,
    )
```

```python
from functools import partial

import jax
import jax.numpy as jnp
from jax import lax
from jax.experimental import pallas as pl
from jax.experimental.pallas import tpu as pltpu
from jax.sharding import PartitionSpec as P

ITERS = 2
HOPS = 3
LEARN_RATE = 0.05
CHUNKS = 4
GROUP = 8
RELAYS = 4


def passed_along(block, axis, distance):
    devices = range(lax.axis_size(axis))
    route = [((i - distance) % len(devices), i) for i in devices]
    return lax.ppermute(block, axis, route)


def split_high_low(values):
    high = values.astype(jnp.bfloat16)
    low = (values - high.astype(jnp.float32)).astype(jnp.bfloat16)
    return high, low


def dot_f32(lhs, rhs, lhs_dim, rhs_dim):
    return lax.dot_general(
        lhs, rhs, (((lhs_dim,), (rhs_dim,)), ((), ())), preferred_element_type=jnp.float32
    )


def grads_kernel(chunks, rows_ref, cols_ref, count_ref, *refs):
    x_refs = refs[:chunks]
    y_ref, ratings_ref = refs[chunks : chunks + 2]
    base_refs = refs[chunks + 2 : 2 * chunks + 2]
    user_ref = refs[2 * chunks + 2]
    group, tile = ratings_ref.shape[0], ratings_ref.shape[-1]
    rank = y_ref.shape[0]
    part_rank = rank // chunks
    first = pl.program_id(0) * group
    total = count_ref[0]

    @pl.when(pl.program_id(0) == 0)
    def _():
        for x_ref, base_ref in zip(x_refs, base_refs):
            base_ref[...] = 0.5 * x_ref[...]
        user_ref[...] = jnp.zeros_like(user_ref)

    @pl.when(first < total)
    def _():
        parts = []
        for k in range(group):
            row = pl.ds(pl.multiple_of(rows_ref[first + k] * tile, tile), tile)
            col = pl.ds(pl.multiple_of(cols_ref[first + k] * tile, tile), tile)
            limit = jnp.where(first + k < total, 1.0, 0.0).astype(jnp.float32)
            x = jnp.concatenate([x_ref[:, row] for x_ref in x_refs], axis=0)
            x_high, x_low = split_high_low(x)
            y_high, y_low = split_high_low(y_ref[:, col])
            rebuilt = dot_f32(
                jnp.concatenate([x_high, x_low, x_high], axis=0),
                jnp.concatenate([y_high, y_high, y_low], axis=0),
                0,
                0,
            )
            clipped = jnp.clip(rebuilt - ratings_ref[k].astype(jnp.float32), -limit, limit)
            c_high, c_low = split_high_low(clipped)
            item_pair = dot_f32(jnp.concatenate([y_high, y_low], axis=0), c_high, 1, 1)
            item_part = item_pair[:rank] + item_pair[rank:] + dot_f32(y_high, c_low, 1, 1)
            user_pair = dot_f32(jnp.concatenate([x_high, x_low], axis=0), c_high, 1, 0)
            user_part = user_pair[:rank] + user_pair[rank:] + dot_f32(x_high, c_low, 1, 0)
            parts.append((row, col, item_part, user_part))
        for row, col, item_part, user_part in parts:
            for c, base_ref in enumerate(base_refs):
                base_ref[:, row] -= LEARN_RATE * item_part[c * part_rank : (c + 1) * part_rank]
            user_ref[:, col] += user_part


def local_grads(x_parts, users_whole, slot_values, row_index, column_index, block_total):
    chunks = len(x_parts)
    slot_total, tile = slot_values.shape[0], slot_values.shape[-1]
    rank, users = users_whole.shape
    items = x_parts[0].shape[1]
    once = pl.Buffered(1)
    x_spec = pl.BlockSpec(x_parts[0].shape, lambda i, *_: (0, 0), pipeline_mode=once)
    y_spec = pl.BlockSpec((rank, users), lambda i, *_: (0, 0), pipeline_mode=once)
    outs = pl.pallas_call(
        partial(grads_kernel, chunks),
        grid_spec=pltpu.PrefetchScalarGridSpec(
            num_scalar_prefetch=3,
            grid=(slot_total // GROUP,),
            in_specs=[x_spec] * chunks
            + [y_spec, pl.BlockSpec((GROUP, tile, tile), lambda i, *_: (i, 0, 0))],
            out_specs=[x_spec] * chunks + [y_spec],
        ),
        out_shape=[jax.ShapeDtypeStruct(p.shape, jnp.float32) for p in x_parts]
        + [jax.ShapeDtypeStruct((rank, users), jnp.float32)],
        compiler_params=pltpu.CompilerParams(vmem_limit_bytes=24 << 20),
        cost_estimate=pl.CostEstimate(
            flops=18 * slot_total * tile * tile * rank,
            bytes_accessed=8 * rank * items + 2 * slot_total * tile * tile,
            transcendentals=0,
        ),
    )(row_index, column_index, block_total, *x_parts, users_whole, slot_values)
    return outs[:chunks], outs[chunks]


def two_steps(hops, item_here, user_here, slot_values, row_index, column_index, block_total):
    rank = item_here.shape[0]
    size = rank // CHUNKS
    x_parts = [item_here[c * size : (c + 1) * size] for c in range(CHUNKS)]
    for hop in hops:
        peers = [passed_along(part, "site", -(1 << hop)) for part in x_parts]
        users_whole = lax.all_gather(user_here, "item", axis=1, tiled=True)
        bases, user_grad = local_grads(
            x_parts, users_whole, slot_values, row_index, column_index, block_total
        )
        x_parts = [base + 0.5 * peer for base, peer in zip(bases, peers)]
        owned = lax.psum_scatter(user_grad, "item", scatter_dimension=1, tiled=True)
        user_here = user_here - LEARN_RATE * owned
    return jnp.concatenate(x_parts, axis=0), user_here


def mix_kernel(hops, xs, bases, x1_first, x1s, q_lands, p_lands, hop_a, hop_b, *sems):
    p_send, p_recv, q_send, q_recv, r_a, r_b, f_a, f_b = sems
    site, item = lax.axis_index("site"), lax.axis_index("item")
    sites = lax.axis_size("site")
    place = lax.rem(site, RELAYS)
    layer = site - place
    ahead = lax.rem(site + sites - RELAYS, sites)
    behind = lax.rem(site + RELAYS, sites)
    width = x1_first.shape[1] // 2
    part = width // RELAYS
    steps = 2 * len(xs)

    def view(ref, j):
        return ref.at[:, pl.ds((j % 2) * width, width)]

    def slab(ref, j, q):
        return ref.at[:, pl.ds((j % 2) * width + q * part, part)]

    def copy(src, dst, send, recv, target):
        return pltpu.make_async_remote_copy(
            src_ref=src,
            dst_ref=dst,
            send_sem=send,
            recv_sem=recv,
            device_id=(item, target),
            device_id_type=pl.DeviceIdType.MESH,
        )

    barrier = pltpu.get_barrier_semaphore()
    peers = [layer + lax.rem(place + k, RELAYS) for k in range(1, RELAYS)] + [ahead, behind]
    for peer in peers:
        pl.semaphore_signal(
            barrier, inc=1, device_id=(item, peer), device_id_type=pl.DeviceIdType.MESH
        )
    pl.semaphore_wait(barrier, len(peers))

    q_sources = [x1_first] + list(x1s[:-1])

    def whole(flow, j):
        src, land, send, recv = (
            (xs[j // 2], p_lands[j // 2], p_send, p_recv)
            if flow == 0
            else (q_sources[j // 2], q_lands[j // 2], q_send, q_recv)
        )
        return src, land, send.at[j], recv.at[j]

    def send(flow, j):
        src, land, send_sem, recv_sem = whole(flow, j)
        if hops[flow] != 0:
            copy(view(src, j), view(land, j), send_sem, recv_sem, ahead).start()
            return

        @pl.when(place != 0)
        def _():
            copy(view(src, j), view(land, j), send_sem, recv_sem, site - 1).start()

        @pl.when(place == 0)
        def _():
            copy(slab(src, j, 0), hop_b.at[j], send_sem, r_b.at[j], ahead).start()
            for q in range(1, RELAYS):
                copy(slab(src, j, q), hop_a.at[j], send_sem, r_a.at[j], site + q).start()

    def relay(flow, j):
        if hops[flow] != 0:
            return
        _, land, _, recv_sem = whole(flow, j)
        last = RELAYS - 1

        @pl.when(place != 0)
        def _():
            copy(hop_a.at[j], hop_a.at[j], f_a.at[j], r_a.at[j], ahead).wait_recv()

        @pl.when(jnp.logical_and(place != 0, place != last))
        def _():
            copy(hop_a.at[j], hop_b.at[j], f_a.at[j], r_b.at[j], ahead).start()

        @pl.when(place == last)
        def _():
            copy(hop_a.at[j], slab(land, j, last), f_a.at[j], recv_sem, ahead).start()

        for q in range(last):

            @pl.when(place == q)
            def _():
                copy(hop_b.at[j], hop_b.at[j], f_b.at[j], r_b.at[j], ahead).wait_recv()
                copy(
                    hop_b.at[j], slab(land, j, q), f_b.at[j], recv_sem, layer + last
                ).start()

    def relayed(flow, j):
        if hops[flow] != 0:
            return

        @pl.when(place != 0)
        def _():
            copy(hop_a.at[j], hop_a.at[j], f_a.at[j], r_a.at[j], ahead).wait_send()

        @pl.when(place != RELAYS - 1)
        def _():
            copy(hop_b.at[j], hop_b.at[j], f_b.at[j], r_b.at[j], ahead).wait_send()

    def waiter(flow, j):
        src, land, send_sem, recv_sem = whole(flow, j)
        return copy(view(src, j), view(land, j), send_sem, recv_sem, ahead)

    send(0, 0)
    send(1, 0)
    for j in range(steps):
        if j + 1 < steps:
            if j >= 1:
                waiter(0, j - 1).wait_send()
            send(0, j + 1)
        relay(0, j)
        waiter(0, j).wait_recv()
        cols = pl.ds((j % 2) * width, width)
        c = j // 2
        x1s[c][:, cols] = bases[c][:, cols] + 0.5 * p_lands[c][:, cols]
        if j + 1 < steps:
            if j >= 1:
                waiter(1, j - 1).wait_send()
            send(1, j + 1)
        relay(1, j)
    waiter(0, steps - 2).wait_send()
    waiter(0, steps - 1).wait_send()
    waiter(1, steps - 2).wait_send()
    waiter(1, steps - 1).wait_send()
    for j in range(steps):
        relayed(0, j)
        relayed(1, j)
        waiter(1, j).wait_recv()


def mix(hops, xs, bases, x1_first):
    n = len(xs)
    rows, items = x1_first.shape
    steps = 2 * n

    def body(*refs):
        refs = list(refs)
        take = lambda k: [refs.pop(0) for _ in range(k)]
        x, base = take(n), take(n)
        (first,) = take(1)
        x1, q_land, p_land = take(n), take(n), take(n)
        mix_kernel(hops, x, base, first, x1, q_land, p_land, *refs)

    whole_spec = pl.BlockSpec(memory_space=pltpu.VMEM)
    chunk = jax.ShapeDtypeStruct((rows, items), jnp.float32)
    relay_shape = pltpu.VMEM((steps, rows, items // (2 * RELAYS)), jnp.float32)
    outs = pl.pallas_call(
        body,
        out_shape=[chunk] * (2 * n),
        in_specs=[whole_spec] * (2 * n + 1),
        out_specs=[whole_spec] * (2 * n),
        scratch_shapes=[pltpu.VMEM((rows, items), jnp.float32)] * n
        + [relay_shape, relay_shape]
        + [pltpu.SemaphoreType.DMA((steps,))] * 8,
        compiler_params=pltpu.CompilerParams(
            collective_id=1 + hops[0], has_side_effects=True, vmem_limit_bytes=32 << 20
        ),
    )(*xs, *bases, x1_first)
    return outs[:n], outs[n:]


def two_steps_mixed(hops, item_here, user_here, slot_values, row_index, column_index, block_total):
    rank = item_here.shape[0]
    size = rank // CHUNKS
    grads = lambda parts, users: local_grads(
        parts, users, slot_values, row_index, column_index, block_total
    )
    x_parts = [item_here[c * size : (c + 1) * size] for c in range(CHUNKS)]
    peer_first = passed_along(x_parts[0], "site", -(1 << hops[0]))
    users_whole = lax.all_gather(user_here, "item", axis=1, tiled=True)
    bases, user_grad = grads(x_parts, users_whole)
    owned = lax.psum_scatter(user_grad, "item", scatter_dimension=1, tiled=True)
    x1_first = bases[0] + 0.5 * peer_first
    x1_rest, q_parts = mix(hops, x_parts[1:], bases[1:], x1_first)
    peer_last = passed_along(x1_rest[-1], "site", -(1 << hops[1]))
    user_here = user_here - LEARN_RATE * owned
    users_whole = lax.all_gather(user_here, "item", axis=1, tiled=True)
    bases, user_grad = grads([x1_first, *x1_rest], users_whole)
    owned = lax.psum_scatter(user_grad, "item", scatter_dimension=1, tiled=True)
    ends = [base + 0.5 * peer for base, peer in zip(bases, [*q_parts, peer_last])]
    return jnp.concatenate(ends, axis=0), user_here - LEARN_RATE * owned


def per_device(item_factors, user_factors, ratings, block_rows, block_cols, block_count, hop_steps):
    pairs = [(a, b) for a in range(HOPS) for b in range(HOPS) if a != b]
    first, second = hop_steps[0], hop_steps[1]
    chosen = first * (HOPS - 1) + second - (second > first).astype(jnp.int32)
    item_here, user_here = lax.switch(
        chosen,
        [partial(two_steps_mixed if 1 not in pair else two_steps, pair) for pair in pairs],
        item_factors[0],
        user_factors[0],
        ratings[0, 0],
        block_rows[0, 0],
        block_cols[0, 0],
        block_count[0],
    )
    return (item_here[None], user_here[None])


def solution(mesh):
    return jax.shard_map(
        per_device,
        mesh=mesh,
        in_specs=(
            P("site", None, "item"),
            P("site", None, "item"),
            P("site", "item", None, None, None),
            P("site", "item", None),
            P("site", "item", None),
            P("site", "item"),
            P(),
        ),
        out_specs=(P("site", None, "item"), P("site", None, "item")),
        check_vma=False,
    )
```

```python
from functools import partial

import jax
import jax.numpy as jnp
from jax import lax
from jax.experimental import pallas as pl
from jax.experimental.pallas import tpu as pltpu
from jax.sharding import PartitionSpec as P

ITERS = 2
HOPS = 3
LEARN_RATE = 0.05
CHUNKS = 4
GROUP = 8
RELAYS = 4
KERNEL_WEIGHT = 450
MIX_WEIGHT = 100000
BLEND_STEPS = 8


def passed_along(block, axis, distance):
    devices = range(lax.axis_size(axis))
    route = [((i - distance) % len(devices), i) for i in devices]
    return lax.ppermute(block, axis, route)


def split_high_low(values):
    high = values.astype(jnp.bfloat16)
    low = (values - high.astype(jnp.float32)).astype(jnp.bfloat16)
    return high, low


def dot_f32(lhs, rhs, lhs_dim, rhs_dim):
    return lax.dot_general(
        lhs, rhs, (((lhs_dim,), (rhs_dim,)), ((), ())), preferred_element_type=jnp.float32
    )


def grads_kernel(chunks, rows_ref, cols_ref, count_ref, *refs):
    x_refs = refs[:chunks]
    y_ref, ratings_ref = refs[chunks : chunks + 2]
    base_ref, user_ref = refs[chunks + 2 :]
    group, tile = ratings_ref.shape[0], ratings_ref.shape[-1]
    rank = y_ref.shape[0]
    first = pl.program_id(0) * group
    total = count_ref[0]

    @pl.when(pl.program_id(0) == 0)
    def _():
        start = 0
        for x_ref in x_refs:
            base_ref[start : start + x_ref.shape[0], :] = 0.5 * x_ref[...]
            start += x_ref.shape[0]
        user_ref[...] = jnp.zeros_like(user_ref)

    @pl.when(first < total)
    def _():
        parts = []
        for k in range(group):
            row = pl.ds(pl.multiple_of(rows_ref[first + k] * tile, tile), tile)
            col = pl.ds(pl.multiple_of(cols_ref[first + k] * tile, tile), tile)
            limit = jnp.where(first + k < total, 1.0, 0.0).astype(jnp.float32)
            x = jnp.concatenate([x_ref[:, row] for x_ref in x_refs], axis=0)
            x_high, x_low = split_high_low(x)
            y_high, y_low = split_high_low(y_ref[:, col])
            rebuilt = dot_f32(
                jnp.concatenate([x_high, x_low, x_high], axis=0),
                jnp.concatenate([y_high, y_high, y_low], axis=0),
                0,
                0,
            )
            clipped = jnp.clip(rebuilt - ratings_ref[k].astype(jnp.float32), -limit, limit)
            c_high, c_low = split_high_low(clipped)
            item_pair = dot_f32(jnp.concatenate([y_high, y_low], axis=0), c_high, 1, 1)
            item_part = item_pair[:rank] + item_pair[rank:] + dot_f32(y_high, c_low, 1, 1)
            user_pair = dot_f32(jnp.concatenate([x_high, x_low], axis=0), c_high, 1, 0)
            user_part = user_pair[:rank] + user_pair[rank:] + dot_f32(x_high, c_low, 1, 0)
            parts.append((row, col, item_part, user_part))
        for row, col, item_part, user_part in parts:
            base_ref[:, row] -= LEARN_RATE * item_part
            user_ref[:, col] += user_part


def local_grads(x_parts, users_whole, slot_values, row_index, column_index, block_total):
    chunks = len(x_parts)
    slot_total, tile = slot_values.shape[0], slot_values.shape[-1]
    rank, users = users_whole.shape
    items = x_parts[0].shape[1]
    once = pl.Buffered(1)
    held = lambda shape: pl.BlockSpec(shape, lambda i, *_: (0, 0), pipeline_mode=once)
    return pl.pallas_call(
        partial(grads_kernel, chunks),
        grid_spec=pltpu.PrefetchScalarGridSpec(
            num_scalar_prefetch=3,
            grid=(slot_total // GROUP,),
            in_specs=[held(part.shape) for part in x_parts]
            + [held((rank, users)), pl.BlockSpec((GROUP, tile, tile), lambda i, *_: (i, 0, 0))],
            out_specs=[held((rank, items)), held((rank, users))],
        ),
        out_shape=[
            jax.ShapeDtypeStruct((rank, items), jnp.float32),
            jax.ShapeDtypeStruct((rank, users), jnp.float32),
        ],
        compiler_params=pltpu.CompilerParams(vmem_limit_bytes=24 << 20),
        cost_estimate=pl.CostEstimate(
            flops=KERNEL_WEIGHT * slot_total * tile * tile * rank,
            bytes_accessed=8 * rank * items + 2 * slot_total * tile * tile,
            transcendentals=0,
        ),
    )(row_index, column_index, block_total, *x_parts, users_whole, slot_values)


def over_items(block):
    total = block
    for distance in range(1, lax.axis_size("item")):
        total = total + passed_along(block, "item", distance)
    return total


def owned_part(whole):
    count = lax.axis_size("item")
    width = whole.shape[1] // count
    me = lax.axis_index("item")
    cut = lambda who: lax.dynamic_slice_in_dim(whole, who * width, width, axis=1)
    total = cut(me)
    for distance in range(1, count):
        total = total + passed_along(cut(lax.rem(me + distance, count)), "item", distance)
    return total


def kept_part(whole):
    width = whole.shape[1] // lax.axis_size("item")
    return lax.dynamic_slice_in_dim(whole, lax.axis_index("item") * width, width, axis=1)


def blend_kernel(base_ref, *refs):
    out_ref = refs[-1]
    start = 0
    for ref in refs[:-1]:
        rows = slice(start, start + ref.shape[0])
        out_ref[rows, :] = base_ref[rows, :] + 0.5 * ref[...]
        start += ref.shape[0]


def blend(base, peers):
    rank, items = base.shape
    width = items // BLEND_STEPS
    spec = lambda rows: pl.BlockSpec((rows, width), lambda i: (0, i))
    return pl.pallas_call(
        blend_kernel,
        grid=(BLEND_STEPS,),
        in_specs=[spec(rank)] + [spec(peer.shape[0]) for peer in peers],
        out_specs=spec(rank),
        out_shape=jax.ShapeDtypeStruct((rank, items), jnp.float32),
    )(base, *peers)


def cut_rows(block):
    size = block.shape[0] // CHUNKS
    return [block[c * size : (c + 1) * size] for c in range(CHUNKS)]


def two_steps(hops, item_here, user_here, slot_values, row_index, column_index, block_total):
    grads = lambda parts, users: local_grads(
        parts, users, slot_values, row_index, column_index, block_total
    )
    peers = [passed_along(part, "site", -(1 << hops[0])) for part in cut_rows(item_here)]
    users_whole = lax.all_gather(user_here, "item", axis=1, tiled=True)
    base, user_grad = grads([item_here], users_whole)
    users_whole = users_whole - LEARN_RATE * over_items(user_grad)
    x_parts = [part + 0.5 * peer for part, peer in zip(cut_rows(base), peers)]
    peers = [passed_along(part, "site", -(1 << hops[1])) for part in x_parts]
    base, user_grad = grads(x_parts, users_whole)
    return blend(base, peers), kept_part(users_whole) - LEARN_RATE * owned_part(user_grad)


def mix_kernel(hops, *refs):
    x, base, x1_first, users, grad, x1_mid, x1_last, q_land, users_next = refs[:9]
    p_land, grad_land, hop_a, hop_b, g_send, g_recv = refs[9:15]
    p_send, p_recv, q_send, q_recv, r_a, r_b, f_a, f_b = refs[15:]
    site, item = lax.axis_index("site"), lax.axis_index("item")
    sites = lax.axis_size("site")
    place = lax.rem(site, RELAYS)
    layer = site - place
    ahead = lax.rem(site + sites - RELAYS, sites)
    behind = lax.rem(site + RELAYS, sites)
    rows = x1_first.shape[0]
    width = x1_first.shape[1] // 2
    part = width // RELAYS
    steps = 2 * q_land.shape[0] // rows

    def view(at, j):
        ref, start = at
        return ref.at[pl.ds(start, rows), pl.ds((j % 2) * width, width)]

    def slab(at, j, q):
        ref, start = at
        return ref.at[pl.ds(start, rows), pl.ds((j % 2) * width + q * part, part)]

    def copy(src, dst, send, recv, target):
        return pltpu.make_async_remote_copy(
            src_ref=src,
            dst_ref=dst,
            send_sem=send,
            recv_sem=recv,
            device_id=(item, target),
            device_id_type=pl.DeviceIdType.MESH,
        )

    barrier = pltpu.get_barrier_semaphore()
    peers = [layer + lax.rem(place + k, RELAYS) for k in range(1, RELAYS)] + [ahead, behind]
    for peer in peers:
        pl.semaphore_signal(
            barrier, inc=1, device_id=(item, peer), device_id_type=pl.DeviceIdType.MESH
        )
    pl.semaphore_signal(
        barrier, inc=1, device_id=(1 - item, site), device_id_type=pl.DeviceIdType.MESH
    )
    pl.semaphore_wait(barrier, len(peers) + 1)
    swap = pltpu.make_async_remote_copy(
        src_ref=grad,
        dst_ref=grad_land,
        send_sem=g_send,
        recv_sem=g_recv,
        device_id=(1 - item, site),
        device_id_type=pl.DeviceIdType.MESH,
    )

    def whole(flow, j):
        start = (j // 2) * rows
        if flow == 0:
            return (x, start + rows), (p_land, start), p_send.at[j], p_recv.at[j]
        src = (x1_first, 0) if j < 2 else (x1_mid, start - rows)
        return src, (q_land, start), q_send.at[j], q_recv.at[j]

    def send(flow, j):
        src, land, send_sem, recv_sem = whole(flow, j)
        if hops[flow] != 0:
            copy(view(src, j), view(land, j), send_sem, recv_sem, ahead).start()
            return

        @pl.when(place != 0)
        def _():
            copy(view(src, j), view(land, j), send_sem, recv_sem, site - 1).start()

        @pl.when(place == 0)
        def _():
            copy(slab(src, j, 0), hop_b.at[j], send_sem, r_b.at[j], ahead).start()
            for q in range(1, RELAYS):
                copy(slab(src, j, q), hop_a.at[j], send_sem, r_a.at[j], site + q).start()

    def relay(flow, j):
        if hops[flow] != 0:
            return
        _, land, _, recv_sem = whole(flow, j)
        last = RELAYS - 1

        @pl.when(place != 0)
        def _():
            copy(hop_a.at[j], hop_a.at[j], f_a.at[j], r_a.at[j], ahead).wait_recv()

        @pl.when(jnp.logical_and(place != 0, place != last))
        def _():
            copy(hop_a.at[j], hop_b.at[j], f_a.at[j], r_b.at[j], ahead).start()

        @pl.when(place == last)
        def _():
            copy(hop_a.at[j], slab(land, j, last), f_a.at[j], recv_sem, ahead).start()

        for q in range(last):

            @pl.when(place == q)
            def _():
                copy(hop_b.at[j], hop_b.at[j], f_b.at[j], r_b.at[j], ahead).wait_recv()
                copy(
                    hop_b.at[j], slab(land, j, q), f_b.at[j], recv_sem, layer + last
                ).start()

    def relayed(flow, j):
        if hops[flow] != 0:
            return

        @pl.when(place != 0)
        def _():
            copy(hop_a.at[j], hop_a.at[j], f_a.at[j], r_a.at[j], ahead).wait_send()

        @pl.when(place != RELAYS - 1)
        def _():
            copy(hop_b.at[j], hop_b.at[j], f_b.at[j], r_b.at[j], ahead).wait_send()

    def waiter(flow, j):
        src, land, send_sem, recv_sem = whole(flow, j)
        return copy(view(src, j), view(land, j), send_sem, recv_sem, ahead)

    send(0, 0)
    send(1, 0)
    swap.start()
    for j in range(steps):
        if j + 1 < steps:
            if j >= 1:
                waiter(0, j - 1).wait_send()
            send(0, j + 1)
        relay(0, j)
        waiter(0, j).wait_recv()
        cols = pl.ds((j % 2) * width, width)
        start = (j // 2) * rows
        out, at = (x1_last, 0) if j >= steps - 2 else (x1_mid, start)
        out[at : at + rows, cols] = (
            base[start + rows : start + 2 * rows, cols] + 0.5 * p_land[start : start + rows, cols]
        )
        if j + 1 < steps:
            if j >= 1:
                waiter(1, j - 1).wait_send()
            send(1, j + 1)
        relay(1, j)
    swap.wait()
    users_next[...] = users[...] - LEARN_RATE * (grad[...] + grad_land[...])
    waiter(0, steps - 2).wait_send()
    waiter(0, steps - 1).wait_send()
    waiter(1, steps - 2).wait_send()
    waiter(1, steps - 1).wait_send()
    for j in range(steps):
        relayed(0, j)
        relayed(1, j)
        waiter(1, j).wait_recv()


def mix(hops, x, base, x1_first, users, grad):
    rows, items = x1_first.shape
    rest = x.shape[0] - rows
    steps = 2 * rest // rows
    whole_spec = pl.BlockSpec(memory_space=pltpu.VMEM)
    shape = lambda n: jax.ShapeDtypeStruct((n, items), jnp.float32)
    relay_shape = pltpu.VMEM((steps, rows, items // (2 * RELAYS)), jnp.float32)
    return pl.pallas_call(
        partial(mix_kernel, hops),
        out_shape=[
            shape(rest - rows),
            shape(rows),
            shape(rest),
            jax.ShapeDtypeStruct(users.shape, jnp.float32),
        ],
        in_specs=[whole_spec] * 5,
        out_specs=[whole_spec] * 4,
        scratch_shapes=[
            pltpu.VMEM((rest, items), jnp.float32),
            pltpu.VMEM(users.shape, jnp.float32),
            relay_shape,
            relay_shape,
            pltpu.SemaphoreType.DMA,
            pltpu.SemaphoreType.DMA,
        ]
        + [pltpu.SemaphoreType.DMA((steps,))] * 8,
        compiler_params=pltpu.CompilerParams(
            collective_id=1 + hops[0], has_side_effects=True, vmem_limit_bytes=32 << 20
        ),
        cost_estimate=pl.CostEstimate(
            flops=MIX_WEIGHT * rest * items,
            bytes_accessed=16 * rest * items,
            transcendentals=0,
        ),
    )(x, base, x1_first, users, grad)


def two_steps_mixed(hops, item_here, user_here, slot_values, row_index, column_index, block_total):
    size = item_here.shape[0] // CHUNKS
    grads = lambda parts, users: local_grads(
        parts, users, slot_values, row_index, column_index, block_total
    )
    peer_first = passed_along(item_here[:size], "site", -(1 << hops[0]))
    users_whole = lax.all_gather(user_here, "item", axis=1, tiled=True)
    base, user_grad = grads([item_here], users_whole)
    x1_first = base[:size] + 0.5 * peer_first
    x1_mid, x1_last, q_land, users_whole = mix(
        hops, item_here, base, x1_first, users_whole, user_grad
    )
    peer_last = passed_along(x1_last, "site", -(1 << hops[1]))
    base, user_grad = grads([x1_first, x1_mid, x1_last], users_whole)
    users_out = kept_part(users_whole) - LEARN_RATE * owned_part(user_grad)
    return blend(base, [q_land, peer_last]), users_out


def per_device(item_factors, user_factors, ratings, block_rows, block_cols, block_count, hop_steps):
    mixed = lambda pair: (
        1 not in pair
        and lax.axis_size("item") == 2
        and lax.axis_size("site") % RELAYS == 0
        and lax.axis_size("site") > 2 * RELAYS
    )
    pairs = [(a, b) for a in range(HOPS) for b in range(HOPS) if a != b]
    first, second = hop_steps[0], hop_steps[1]
    chosen = first * (HOPS - 1) + second - (second > first).astype(jnp.int32)
    item_here, user_here = lax.switch(
        chosen,
        [partial(two_steps_mixed if mixed(pair) else two_steps, pair) for pair in pairs],
        item_factors[0],
        user_factors[0],
        ratings[0, 0],
        block_rows[0, 0],
        block_cols[0, 0],
        block_count[0],
    )
    return (item_here[None], user_here[None])


def solution(mesh):
    return jax.shard_map(
        per_device,
        mesh=mesh,
        in_specs=(
            P("site", None, "item"),
            P("site", None, "item"),
            P("site", "item", None, None, None),
            P("site", "item", None),
            P("site", "item", None),
            P("site", "item"),
            P(),
        ),
        out_specs=(P("site", None, "item"), P("site", None, "item")),
        check_vma=False,
    )
```
